32 devices in a mesh: prow: 8 (over z, core), pcol: 4 (over y, x).
Axes of the slice: x: 2, y: 2, z: 4, core: 2. Of those that a mesh axis runs over, the one named last changes fastest.
Arguments:
- leaf_source: bfloat16 [8, 4, 8, 256, 128], P('prow', 'pcol'), may hold values from -6 to 6
- band_source: bfloat16 [8, 256, 128], P('prow'), may hold values from -6 to 6
- strip_source: bfloat16 [4, 256, 128], P('pcol'), may hold values from -6 to 6
- summit_source: bfloat16 [256, 128], replicated, may hold values from -6 to 6
- leaf_inverse: bfloat16 [8, 4, 8, 256, 256], P('prow', 'pcol'), may hold values from -1 to 2
- band_inverse: bfloat16 [8, 256, 256], P('prow'), may hold values from -1 to 2
- strip_inverse: bfloat16 [4, 256, 256], P('pcol'), may hold values from -1 to 2
- summit_inverse: bfloat16 [256, 256], replicated, may hold values from -1 to 2
- leaf_blocks: bfloat16 [8, 4, 28, 256, 256], P('prow', 'pcol'), may hold values from -0.09375 to 0.09375
- band_blocks: bfloat16 [8, 4, 8, 256, 256], P('prow', 'pcol'), may hold values from -0.046875 to 0.046875
- strip_blocks: bfloat16 [8, 4, 8, 256, 256], P('prow', 'pcol'), may hold values from -0.03125 to 0.03125
- summit_blocks: bfloat16 [8, 4, 8, 256, 256], P('prow', 'pcol'), may hold values from -0.046875 to 0.046875
- coupling: bfloat16 [8, 4, 256, 256], P('prow', 'pcol'), may hold values from -0.09375 to 0.09375
- summit_band: bfloat16 [8, 256, 256], P('prow', 'pcol'), may hold values from -0.078125 to 0.078125
- summit_strip: bfloat16 [4, 256, 256], P('pcol'), may hold values from -0.078125 to 0.078125
- parents: int32 [8, 4, 8], P('prow', 'pcol'), may hold values from 1 to 8, as said below
- widths: int32 [8, 4, 8], P('prow', 'pcol'), may hold values from 64 to 256
Outputs:
- leaf_answer: bfloat16 [8, 4, 8, 256, 128], P('prow', 'pcol')
- band_answer: bfloat16 [8, 256, 128], P('prow')
- strip_answer: bfloat16 [4, 256, 128], P('pcol')
- summit_answer: bfloat16 [256, 128], replicated
The draws below stay inside these ranges and needn't reach their ends.
Inputs may be any that keep to these rules, and one draw needn't show every extreme that they name: parents[r, c, a] is a later leaf of the same subtree, or 8 where leaf a links only to the separators.
All inputs are finite; a program needn't handle non-finite values.
Results may differ from the reference program's by a relative error of at most 0.015.
Values sent between devices are 32-bit elements; how exact they have to be, the bound alone decides.
No kernel may reach another device: no remote copies, remote signals or barrier semaphores. Data moves between devices by JAX's collectives and lax.ppermute only.
A program may use at most 64 MiB of HBM per device.

```python
import math
import jax
import jax.numpy as jnp
from jax import lax

COLUMNS = 256
VECTORS = 128
LEAVES = 8
PASSES = 2
LEAF_PAIRS = 28
N_PROW = 8
N_PCOL = 4
DEVICES = 32


def inverse_stack(key, lead):
    shape = lead + (COLUMNS, COLUMNS)
    identity = jnp.eye(COLUMNS, dtype=jnp.float32)
    noise = jnp.clip(jax.random.normal(key, shape, jnp.float32), -4.0, 4.0) * (0.5 / math.sqrt(COLUMNS))
    return (identity + noise).astype(jnp.bfloat16)


def draw_leaf_inverse(key, part):
    return inverse_stack(key, (N_PROW, N_PCOL, LEAVES))


def draw_band_inverse(key, part):
    return inverse_stack(key, (N_PROW,))


def draw_strip_inverse(key, part):
    return inverse_stack(key, (N_PCOL,))


def draw_summit_inverse(key, part):
    return inverse_stack(key, ())


def draw_parents(key, part):
    positions = jnp.arange(LEAVES, dtype=jnp.int32)
    raw_bits = jax.random.randint(key, (N_PROW, N_PCOL, LEAVES), 0, 1 << 20, dtype=jnp.int32)
    return positions + 1 + raw_bits % (LEAVES - positions)


def set_ends(values, own_key, low, top_value):
    longest = values.shape.index(max(values.shape))
    spots = []
    for shift in (0, 1):
        where = [jax.random.randint(jax.random.fold_in(own_key, axis), (), 0, length) for axis, length in enumerate(values.shape)]
        where[longest] = (where[longest] + shift) % values.shape[longest]
        spots.append(tuple(where))
    return values.at[spots[0]].set(low).at[spots[1]].set(top_value)


def shard_levels(own_key, extent, shards, least, top_value):
    def one(dim, parts):
        steps = jax.random.uniform(jax.random.fold_in(jax.random.fold_in(own_key, 6), dim), (parts,), jnp.float32, least / len(shards), top_value / len(shards))
        return jnp.repeat(jnp.exp(steps), extent[dim] // parts).reshape((-1,) + (1,) * (len(extent) - dim - 1))

    level = one(*shards[0])
    for cut in shards[1:]:
        level = level * one(*cut)
    return level


def normal_values(own_key, dims, spread, most, split=(), held_as=jnp.bfloat16):
    drawn = spread * jax.random.normal(own_key, dims, jnp.float32)
    if split:
        drawn = drawn * shard_levels(own_key, dims, split, -0.22, 0.18)
    return jnp.clip(drawn, -most, most).astype(held_as)


def setup_inputs(seed: int = 0) -> dict:
    key_list = jax.random.split(jax.random.key(seed), 18)
    return {
        "leaf_source": normal_values(key_list[0], (N_PROW, N_PCOL, LEAVES, COLUMNS, VECTORS), 1.0, 6.0, ((0, 8), (1, 4))),
        "band_source": normal_values(key_list[1], (N_PROW, COLUMNS, VECTORS), 1.0, 6.0, ((0, 8),)),
        "strip_source": normal_values(key_list[2], (N_PCOL, COLUMNS, VECTORS), 1.0, 6.0, ((0, 4),)),
        "summit_source": normal_values(key_list[3], (COLUMNS, VECTORS), 1.0, 6.0),
        "leaf_inverse": draw_leaf_inverse(jax.random.fold_in(key_list[17], 71), 0),
        "band_inverse": draw_band_inverse(jax.random.fold_in(key_list[17], 71), 0),
        "strip_inverse": draw_strip_inverse(jax.random.fold_in(key_list[17], 71), 0),
        "summit_inverse": draw_summit_inverse(jax.random.fold_in(key_list[17], 71), 0),
        "leaf_blocks": normal_values(key_list[8], (N_PROW, N_PCOL, LEAF_PAIRS, COLUMNS, COLUMNS), (2 * COLUMNS * LEAVES) ** -0.5, 0.09375, ((0, 8), (1, 4))),
        "band_blocks": normal_values(key_list[9], (N_PROW, N_PCOL, LEAVES, COLUMNS, COLUMNS), (2 * COLUMNS * N_PCOL * LEAVES) ** -0.5, 0.046875, ((0, 8), (1, 4))),
        "strip_blocks": normal_values(key_list[10], (N_PROW, N_PCOL, LEAVES, COLUMNS, COLUMNS), (2 * COLUMNS * N_PROW * LEAVES) ** -0.5, 0.03125, ((0, 8), (1, 4))),
        "summit_blocks": normal_values(key_list[11], (N_PROW, N_PCOL, LEAVES, COLUMNS, COLUMNS), (COLUMNS * DEVICES * LEAVES // 4) ** -0.5, 0.046875, ((0, 8), (1, 4))),
        "coupling": normal_values(key_list[12], (N_PROW, N_PCOL, COLUMNS, COLUMNS), (2 * COLUMNS * N_PROW) ** -0.5, 0.09375, ((0, 8), (1, 4))),
        "summit_band": normal_values(key_list[13], (N_PROW, COLUMNS, COLUMNS), (2 * COLUMNS * (N_PROW + N_PCOL)) ** -0.5, 0.078125, ((0, 8), (1, 4))),
        "summit_strip": normal_values(key_list[14], (N_PCOL, COLUMNS, COLUMNS), (2 * COLUMNS * (N_PROW + N_PCOL)) ** -0.5, 0.078125, ((0, 4),)),
        "parents": draw_parents(jax.random.fold_in(key_list[17], 71), 0),
        "widths": set_ends(jax.random.randint(key_list[16], (N_PROW, N_PCOL, LEAVES), COLUMNS // 4, COLUMNS + 1), jax.random.fold_in(key_list[16], 1), COLUMNS // 4, COLUMNS).astype(jnp.int32),
    }


def ancestors(parent_list, leaf_count):
    node_ids = jnp.arange(leaf_count + 1, dtype=jnp.int32)
    current = parent_list.astype(jnp.int32)
    extended = jnp.concatenate([current, jnp.full((1,), leaf_count, jnp.int32)])
    reached = jnp.zeros((leaf_count + 1, leaf_count), jnp.float32)
    for repeat in range(leaf_count):
        matches = current[None, :] == node_ids[:, None]
        reached = jnp.maximum(reached, matches.astype(jnp.float32))
        current = jnp.sum(jnp.where(matches, extended[:, None], 0), axis=0).astype(jnp.int32)
    return reached[:leaf_count]


def product(left, right, form):
    return jnp.einsum(form, left.astype(jnp.float32), right.astype(jnp.float32), precision=lax.Precision.HIGHEST)


def forward_block(inverse, source, partial_value):
    residual = (source.astype(jnp.float32) - partial_value).astype(jnp.bfloat16)
    return product(inverse, residual, "ij,jr->ir").astype(jnp.bfloat16)


def backward_block(inverse, source, partial_value):
    residual = (source.astype(jnp.float32) - partial_value).astype(jnp.bfloat16)
    return product(inverse, residual, "ji,jr->ir").astype(jnp.bfloat16)


def leaf_forward(pair_blocks, inverses, sources, reached, row_mask):
    leaf_count = sources.shape[0]
    solved = []
    for position in range(leaf_count):
        residual = sources[position].astype(jnp.float32)
        if position > 0:
            first_pair = position * (position - 1) // 2
            weights = reached[position, :position]
            stacked = jnp.stack(solved).astype(jnp.float32) * weights[:, None, None]
            residual = residual - product(pair_blocks[first_pair:first_pair + position], stacked, "bij,bjr->ir")
        residual = (row_mask[position] * residual).astype(jnp.bfloat16)
        solved.append((row_mask[position] * product(inverses[position], residual, "ij,jr->ir")).astype(jnp.bfloat16))
    return jnp.stack(solved)


def leaf_backward(pair_blocks, inverses, solved, outer, reached, row_mask):
    leaf_count = solved.shape[0]
    pending = outer
    answers = [None] * leaf_count
    for position in reversed(range(leaf_count)):
        residual = (row_mask[position] * (solved[position].astype(jnp.float32) - pending[position])).astype(jnp.bfloat16)
        update = (row_mask[position] * product(inverses[position], residual, "ji,jr->ir")).astype(jnp.bfloat16)
        answers[position] = update
        if position > 0:
            first_pair = position * (position - 1) // 2
            pushed = product(pair_blocks[first_pair:first_pair + position], update, "bji,jr->bir")
            pending = pending.at[:position].add(reached[position, :position][:, None, None] * pushed)
    return jnp.stack(answers)


def reference(leaf_source, band_source, strip_source, summit_source, leaf_inverse, band_inverse, strip_inverse, summit_inverse, leaf_blocks, band_blocks, strip_blocks, summit_blocks, coupling, summit_band, summit_strip, parents, widths):
    grid_count = N_PROW * N_PCOL

    def flatten(array):
        return array.reshape((grid_count,) + array.shape[2:])

    column_ids = jnp.arange(COLUMNS, dtype=jnp.int32)

    def masks_of(width_list):
        return (column_ids[None, :] < width_list[:, None]).astype(jnp.float32)[:, :, None]

    leaf_inputs = tuple(flatten(array) for array in (leaf_inverse, leaf_blocks, band_blocks, strip_blocks, summit_blocks, parents, widths))
    current = (leaf_source, band_source, strip_source, summit_source)
    for iteration in range(PASSES):
        leaf_now, band_now, strip_now, summit_now = current

        def forward_one(items):
            inverse, pairs, to_band, to_strip, to_summit, parent_one, width_one, source = items
            reached = ancestors(parent_one, LEAVES)
            solved = leaf_forward(pairs, inverse, source, reached, masks_of(width_one))
            return (solved, product(to_band, solved, "aij,ajr->ir"), product(to_strip, solved, "aij,ajr->ir"), product(to_summit, solved, "aij,ajr->ir"))

        solved, band_terms, strip_terms, summit_terms = lax.map(forward_one, leaf_inputs + (flatten(leaf_now),))
        band_partial = band_terms.reshape(N_PROW, N_PCOL, COLUMNS, VECTORS).sum(axis=1)
        band_solved = jax.vmap(forward_block)(band_inverse, band_now, band_partial)
        strip_partial = strip_terms.reshape(N_PROW, N_PCOL, COLUMNS, VECTORS).sum(axis=0) + product(coupling, band_solved, "rcij,rjn->cin")
        strip_solved = jax.vmap(forward_block)(strip_inverse, strip_now, strip_partial)
        summit_partial = summit_terms.sum(axis=0) + product(summit_band, band_solved, "rki,rkn->in") + product(summit_strip, strip_solved, "cki,ckn->in")
        summit_solved = forward_block(summit_inverse, summit_now, summit_partial)
        summit_answer = backward_block(summit_inverse, summit_solved, jnp.zeros((COLUMNS, VECTORS), jnp.float32))
        strip_answer = jax.vmap(backward_block)(strip_inverse, strip_solved, product(summit_strip, summit_answer, "cki,in->ckn"))
        band_back = product(coupling, strip_answer, "rcji,cjn->rin") + product(summit_band, summit_answer, "rki,in->rkn")
        band_answer = jax.vmap(backward_block)(band_inverse, band_solved, band_back)
        band_each = jnp.broadcast_to(band_answer[:, None], (N_PROW, N_PCOL, COLUMNS, VECTORS)).reshape(grid_count, COLUMNS, VECTORS)
        strip_each = jnp.broadcast_to(strip_answer[None], (N_PROW, N_PCOL, COLUMNS, VECTORS)).reshape(grid_count, COLUMNS, VECTORS)

        def backward_one(items):
            inverse, pairs, to_band, to_strip, to_summit, parent_one, width_one, solved_one, band_one, strip_one = items
            reached = ancestors(parent_one, LEAVES)
            outer = product(to_band, band_one, "aij,ir->ajr") + product(to_strip, strip_one, "aij,ir->ajr") + product(to_summit, summit_answer, "aij,ir->ajr")
            return leaf_backward(pairs, inverse, solved_one, outer, reached, masks_of(width_one))

        leaf_answer = lax.map(backward_one, leaf_inputs + (solved, band_each, strip_each)).reshape(leaf_source.shape)
        current = (leaf_answer, band_answer, strip_answer, summit_answer)
    return current[0], current[1], current[2], current[3]
```

```python
import functools

import jax
import jax.numpy as jnp
from jax import lax
from jax.experimental import pallas as pl
from jax.experimental.pallas import tpu as pltpu
from jax.sharding import PartitionSpec as P

PASSES = 2
F32, BF = jnp.float32, jnp.bfloat16
VMEM = pl.BlockSpec(memory_space=pltpu.VMEM)
SMEM = pl.BlockSpec(memory_space=pltpu.SMEM)
ANY = pl.BlockSpec(memory_space=pl.ANY)


def by(rows, weights):
    return lax.dot_general(rows, weights, (((1,), (0,)), ((), ())), preferred_element_type=F32)


def by_t(rows, weights):
    return lax.dot_general(rows, weights, (((1,), (1,)), ((), ())), preferred_element_type=F32)


def fill_ancestors(parents, ancestors, leaves):
    ancestors[leaves] = 0
    for b in reversed(range(leaves)):
        ancestors[b] = jnp.left_shift(1, parents[b]) | ancestors[parents[b]]


def reach(ancestors, a, b):
    return (jnp.right_shift(ancestors[b], a) & 1).astype(F32)


def mask_of(widths, a, size):
    return (lax.broadcasted_iota(jnp.int32, (1, size), 1) < widths[a]).astype(F32)


def pair(a, b):
    return a * (a - 1) // 2 + b


class Weights:
    def __init__(self, sources, buffers, sems):
        self.sources, self.buffers, self.sems = sources, buffers, sems
        self.copies, self.waited, self.count = {}, set(), 0

    def start(self, name, first, count=1):
        src, dst = self.sources[name], self.buffers[name]
        copy = pltpu.make_async_copy(
            src.at[pl.ds(first, count)], dst.at[pl.ds(first, count)], self.sems.at[self.count]
        )
        self.count += 1
        copy.start()
        for i in range(first, first + count):
            self.copies[name, i] = copy

    def get(self, name, i):
        copy = self.copies[name, i]
        if id(copy) not in self.waited:
            self.waited.add(id(copy))
            copy.wait()
        return self.buffers[name][i]


LINKS = ("band", "strip", "summit")


def forward(w, leaves, source, widths, ancestors, pending, totals, solved):
    size = pending.shape[2]

    def push(a, b, rows):
        term = reach(ancestors, a, b) * by_t(rows, w.get("pair", pair(a, b)))
        if b:
            pending[a] += term
        else:
            pending[a] = term

    def sides(b):
        rows = solved[b]
        for a in range(b + 2, leaves):
            push(a, b, rows)
        for i, name in enumerate(LINKS):
            term = by_t(rows, w.get(name, b))
            if b:
                totals[i] += term
            else:
                totals[i] = term

    for b in range(leaves):
        mask = mask_of(widths, b, size)
        rows = source(b)
        if b:
            rows = rows - pending[b]
        rows = (mask * rows).astype(BF)
        rows = (mask * by_t(rows, w.get("inverse", b))).astype(BF)
        solved[b] = rows
        if b:
            sides(b - 1)
        if b + 1 < leaves:
            push(b + 1, b, rows)
    sides(leaves - 1)


def backward(w, leaves, tops, solved, widths, ancestors, pending, answer):
    size = pending.shape[2]

    def outer(a):
        return sum(by(top, w.get(name, a)) for top, name in zip(tops, LINKS))

    def push(a, b, rows):
        pending[b] += reach(ancestors, a, b) * by(rows, w.get("pair", pair(a, b)))

    pending[leaves - 1] = outer(leaves - 1)
    for a in reversed(range(leaves)):
        mask = mask_of(widths, a, size)
        rows = (mask * (solved[a].astype(F32) - pending[a])).astype(BF)
        rows = (mask * by(rows, w.get("inverse", a))).astype(BF)
        answer[a] = rows
        if a:
            pending[a - 1] = outer(a - 1) if a == leaves - 1 else pending[a - 1] + outer(a - 1)
            push(a, a - 1, rows)
        for b in range(a - 1):
            term = reach(ancestors, a, b) * by(rows, w.get("pair", pair(a, b)))
            if a == leaves - 1:
                pending[b] = term
            else:
                pending[b] += term


def send_pieces(place, totals, sources, outs):
    peers = len(outs)
    part = totals.shape[1] // peers
    r, c = place[0], place[1]
    counted = (c == 0, r == 0, (r == 0) & (c == 0))
    for i, (here, source) in enumerate(zip(counted, sources)):

        @pl.when(here)
        def _(i=i, source=source):
            totals[i] -= source()

    for m, out in enumerate(outs):
        rows = pl.ds(pl.multiple_of((c ^ m) * part, part), part)
        for i in range(3):
            out[pl.ds(i * part, part)] = totals[i, rows]


def join_pieces(place, pieces, tops):
    part = tops.shape[1] // len(pieces)
    for m, piece in enumerate(pieces):
        rows = pl.ds(pl.multiple_of((place[1] ^ m) * part, part), part)
        for i in range(3):
            tops[i, rows] = piece[pl.ds(i * part, part)]


def first_kernel(n, place, parents, widths, leaf_source, band_source, strip_source, summit_source, *refs):
    sources, refs = refs[:5], refs[5:]
    outs, solved, refs = refs[:n], refs[n], refs[n + 1 :]
    buffers, (pending, totals, ancestors, sems) = refs[:5], refs[5:]
    names = ("inverse", "pair") + LINKS
    w = Weights(dict(zip(names, sources)), dict(zip(names, buffers)), sems)
    leaves = leaf_source.shape[0]
    start_forward(w, leaves)
    fill_ancestors(parents, ancestors, leaves)
    forward(w, leaves, lambda b: leaf_source[b].astype(F32).T, widths, ancestors, pending, totals, solved)
    send_pieces(
        place,
        totals,
        [lambda ref=ref: ref[...].astype(F32).T for ref in (band_source, strip_source, summit_source)],
        outs,
    )


def start_forward(w, leaves):
    for b in range(leaves):
        w.start("inverse", b)
        if b + 1 < leaves:
            w.start("pair", pair(b + 1, b))
        for a in range(b + 2, leaves):
            w.start("pair", pair(a, b))
        for name in LINKS:
            w.start(name, b)


def start_backward(w, leaves):
    for a in reversed(range(leaves)):
        for name in LINKS:
            w.start(name, a)
        w.start("inverse", a)
        if a:
            w.start("pair", pair(a, 0), a)


def middle_kernel(n, last, place, parents, widths, solved_before, *refs):
    pieces, sources, refs = refs[:n], refs[n : n + 5], refs[n + 5 :]
    if last:
        leaf_answer, *top_answers = refs[:4]
        refs = refs[4:]
    else:
        outs, solved, refs = refs[:n], refs[n], refs[n + 1 :]
    buffers, (pending, totals, tops, answer, ancestors, sems) = refs[:5], refs[5:]
    names = ("inverse", "pair") + LINKS
    w = Weights(dict(zip(names, sources)), dict(zip(names, buffers)), sems)
    leaves = solved_before.shape[0]
    start_backward(w, leaves)
    fill_ancestors(parents, ancestors, leaves)
    join_pieces(place, pieces, tops)
    rows = [tops[i].astype(BF) for i in range(3)]
    backward(w, leaves, rows, solved_before, widths, ancestors, pending, answer)
    if last:
        for a in range(leaves):
            leaf_answer[a] = answer[a].astype(F32).T.astype(BF)
        for i, out in enumerate(top_answers):
            out[...] = tops[i].T.astype(BF)
    else:
        forward(w, leaves, lambda b: answer[b].astype(F32), widths, ancestors, pending, totals, solved)
        send_pieces(place, totals, [lambda i=i: tops[i] for i in range(3)], outs)


def band_kernel(n, place, inverse, lift, *refs):
    pieces, links, (solved, keep, send), (both,) = refs[:n], refs[n : 2 * n], refs[2 * n : 2 * n + 3], refs[2 * n + 3 :]
    part = solved.shape[0]
    half = keep.shape[0]

    def block(piece, i):
        return piece[pl.ds(i * part, part)]

    partial = sum(block(piece, 0) for piece in pieces)
    rows = by_t((-partial).astype(BF), inverse[...]).astype(BF)
    solved[...] = rows
    for m in range(n):
        both[pl.ds(m * part, part)] = block(pieces[m], 1) + by_t(rows, links[m][...])
    both[pl.ds(n * part, part)] = sum(block(piece, 2) for piece in pieces) + by(rows, lift[...])
    if 2 * half > (n + 1) * part:
        both[pl.ds((n + 1) * part, 2 * half - (n + 1) * part)] = jnp.zeros((2 * half - (n + 1) * part, both.shape[1]), F32)
    core = place[0] & 1
    keep[...] = both[pl.ds(pl.multiple_of(core * half, 8), half)]
    send[...] = both[pl.ds(pl.multiple_of((1 - core) * half, 8), half)]


def top_kernel(n, place, inverse, lift, summit_inverse, solved, mine, other, *refs):
    links, inverses, lifts = refs[:n], refs[n : 2 * n], refs[2 * n : 3 * n]
    outs, (both,) = refs[3 * n : 4 * n], refs[4 * n :]
    half = mine.shape[0]
    part = solved.shape[0]
    core = place[0] & 1
    both[pl.ds(pl.multiple_of(core * half, 8), half)] = mine[...]
    both[pl.ds(pl.multiple_of((1 - core) * half, 8), half)] = other[...]
    strips = [
        by_t((-both[pl.ds(m * part, part)]).astype(BF), inverses[m][...]).astype(BF) for m in range(n)
    ]
    partial = both[pl.ds(n * part, part)] + sum(by(strips[m], lifts[m][...]) for m in range(n))
    summit = by_t((-partial).astype(BF), summit_inverse[...]).astype(BF)
    summit = by(summit, summit_inverse[...]).astype(BF)
    answers = [
        by((strips[m].astype(F32) - by_t(summit, lifts[m][...])).astype(BF), inverses[m][...]).astype(BF)
        for m in range(n)
    ]
    back = by_t(summit, lift[...]) + sum(by(answers[m], links[m][...]) for m in range(n))
    band = by((solved[...].astype(F32) - back).astype(BF), inverse[...]).astype(BF)
    for m in range(n):
        outs[m][pl.ds(0, part)] = band.astype(F32)
        outs[m][pl.ds(part, part)] = answers[m].astype(F32)
        outs[m][pl.ds(2 * part, part)] = summit.astype(F32)


def gather_kernel(n, place, slab, *refs):
    pieces, links, lift = refs[: n - 1], refs[n - 1 : 2 * n - 2], refs[2 * n - 2]
    rows = slab.shape[0]
    size = lift.shape[0]
    for m in range(n):
        spot = pl.ds(pl.multiple_of((place[1] ^ m) * rows, rows), rows)
        if m:
            links[m - 1][...] = pieces[m - 1][pl.ds(0, size)].astype(BF)
            lift[spot] = pieces[m - 1][pl.ds(size, rows)].astype(BF)
        else:
            lift[spot] = slab[...]


def sort_kernel(n, place, *refs):
    k = n - 1
    mine, other, inverses, lifts = refs[:k], refs[k : 2 * k], refs[2 * k : 3 * k], refs[3 * k :]

    @pl.when(place[0] & 1 == 0)
    def _():
        for m in range(k):
            inverses[m][...] = mine[m][...].astype(BF)
            lifts[m][...] = other[m][...].astype(BF)

    @pl.when(place[0] & 1 == 1)
    def _():
        for m in range(k):
            inverses[m][...] = other[m][...].astype(BF)
            lifts[m][...] = mine[m][...].astype(BF)


def cost(flops, moved):
    return pl.CostEstimate(flops=int(flops), bytes_accessed=int(moved), transcendentals=0)


def shape_of(shape, dtype):
    return jax.ShapeDtypeStruct(tuple(shape), dtype)


def swap(array, axis, mask, size):
    return lax.ppermute(array, axis, [(i, i ^ mask) for i in range(size)])


def spread(arrays, size):
    order = sorted(range(1, size), key=lambda m: -bin(m).count("1"))
    got = {m: swap(arrays[m - 1], "pcol", m, size) for m in order}
    return [got[m] for m in range(1, size)]


def per_device(
    n_prow,
    n,
    leaf_source,
    band_source,
    strip_source,
    summit_source,
    leaf_inverse,
    band_inverse,
    strip_inverse,
    summit_inverse,
    leaf_blocks,
    band_blocks,
    strip_blocks,
    summit_blocks,
    coupling,
    summit_band,
    summit_strip,
    parents,
    widths,
):
    leaves, size, vectors = leaf_source.shape[2:]
    pairs = leaf_blocks.shape[2]
    part = vectors // n
    half = -(-(n + 1) * part // 16) * 8
    place = jnp.stack([lax.axis_index("prow"), lax.axis_index("pcol")]).astype(jnp.int32)
    block = (size, size)
    leaf_weights = (leaf_inverse[0, 0], leaf_blocks[0, 0], band_blocks[0, 0], strip_blocks[0, 0], summit_blocks[0, 0])
    buffers = [pltpu.VMEM((count,) + block, BF) for count in (leaves, pairs, leaves, leaves, leaves)]
    n_copies = 4 * leaves + pairs
    scratch = buffers + [pltpu.VMEM((leaves, vectors, size), F32), pltpu.VMEM((3, vectors, size), F32)]
    ends = [pltpu.SMEM((leaves + 1,), jnp.int32), pltpu.SemaphoreType.DMA((n_copies,))]
    pieces = [shape_of((3 * part, size), F32)] * n
    solved_shape = shape_of((leaves, vectors, size), BF)
    sweep_flops = 2 * vectors * size * size * (pairs + 4 * leaves)
    weight_bytes = 2 * size * size * (pairs + 4 * leaves)
    lists = (parents[0, 0], widths[0, 0])

    link_out = jnp.concatenate([coupling[0, 0], summit_band[0]], 0).astype(F32)
    link_in = spread([link_out] * (n - 1), n)
    core = place[0] & 1
    strip_out = jnp.where(core == 0, strip_inverse[0], summit_strip[0]).astype(F32)

    *sent, solved = pl.pallas_call(
        functools.partial(first_kernel, n),
        out_shape=pieces + [solved_shape],
        in_specs=[SMEM] * 3 + [VMEM] * 4 + [ANY] * 5,
        out_specs=[VMEM] * (n + 1),
        scratch_shapes=scratch + ends,
        cost_estimate=cost(sweep_flops, weight_bytes),
        name="first_sweep",
    )(place, *lists, leaf_source[0, 0], band_source[0], strip_source[0], summit_source, *leaf_weights)

    *links, lift = pl.pallas_call(
        functools.partial(gather_kernel, n),
        out_shape=[shape_of(block, BF)] * n,
        in_specs=[SMEM] + [VMEM] * n,
        out_specs=[VMEM] * n,
        cost_estimate=cost(0, 6 * n * size * size),
        name="gather_links",
    )(place, summit_band[0], *link_in)
    links = [coupling[0, 0]] + links

    for step in range(PASSES):
        last = step == PASSES - 1
        got = list(sent[:1]) + spread(sent[1:], n)
        if step == 0:
            strip_out, got = lax.optimization_barrier((strip_out, got))
            strip_in = spread([strip_out] * (n - 1), n)
            strip_over = [swap(array, "prow", 1, n_prow) for array in strip_in]
            sorted_in = pl.pallas_call(
                functools.partial(sort_kernel, n),
                out_shape=[shape_of(block, BF)] * (2 * n - 2),
                in_specs=[SMEM] + [VMEM] * (2 * n - 2),
                out_specs=[VMEM] * (2 * n - 2),
                cost_estimate=cost(0, 12 * n * size * size),
                name="sort_strips",
            )(place, *strip_in, *strip_over)
            inverses = [strip_inverse[0]] + list(sorted_in[: n - 1])
            lifts = [summit_strip[0]] + list(sorted_in[n - 1 :])
        band_solved, keep, send = pl.pallas_call(
            functools.partial(band_kernel, n),
            out_shape=[shape_of((part, size), BF)] + [shape_of((half, size), F32)] * 2,
            in_specs=[SMEM] + [VMEM] * (2 * n + 2),
            out_specs=[VMEM] * 3,
            scratch_shapes=[pltpu.VMEM((2 * half, size), F32)],
            cost_estimate=cost(2 * part * size * size * (n + 2), 2 * size * size * (n + 2)),
            name="band_solve",
        )(place, band_inverse[0], lift, *got, *links)
        mine = keep + swap(send, "prow", 1, n_prow)
        mask = 2
        while mask < n_prow:
            mine = mine + swap(mine, "prow", mask, n_prow)
            mask *= 2
        other = swap(mine, "prow", 1, n_prow)
        back = pl.pallas_call(
            functools.partial(top_kernel, n),
            out_shape=pieces,
            in_specs=[SMEM] + [VMEM] * (6 + 3 * n),
            out_specs=[VMEM] * n,
            scratch_shapes=[pltpu.VMEM((2 * half, size), F32)],
            cost_estimate=cost(2 * part * size * size * (5 * n + 4), 2 * size * size * (3 * n + 3)),
            name="top_solve",
        )(place, band_inverse[0], lift, summit_inverse, band_solved, mine, other, *links, *inverses, *lifts)
        tops = list(back[:1]) + spread(back[1:], n)
        if last:
            shapes = [shape_of((leaves, size, vectors), BF)] + [shape_of((size, vectors), BF)] * 3
        else:
            shapes = pieces + [solved_shape]
        results = pl.pallas_call(
            functools.partial(middle_kernel, n, last),
            out_shape=shapes,
            in_specs=[SMEM] * 3 + [VMEM] * (n + 1) + [ANY] * 5,
            out_specs=[VMEM] * len(shapes),
            scratch_shapes=scratch
            + [pltpu.VMEM((3, vectors, size), F32), pltpu.VMEM((leaves, vectors, size), BF)]
            + ends,
            cost_estimate=cost(sweep_flops * (1 if last else 2), weight_bytes),
            name="last_sweep" if last else "middle_sweep",
        )(place, *lists, solved, *tops, *leaf_weights)
        if not last:
            *sent, solved = results
    leaf_answer, band_answer, strip_answer, summit_answer = results
    return leaf_answer[None, None], band_answer[None], strip_answer[None], summit_answer


def solution(mesh):
    placed = (
        P("prow", "pcol", None, None, None),
        P("prow", None, None),
        P("pcol", None, None),
        P(),
        P("prow", "pcol", None, None, None),
        P("prow", None, None),
        P("pcol", None, None),
        P(),
        P("prow", "pcol", None, None, None),
        P("prow", "pcol", None, None, None),
        P("prow", "pcol", None, None, None),
        P("prow", "pcol", None, None, None),
        P("prow", "pcol", None, None),
        P("prow", "pcol", None),
        P("pcol", None, None),
        P("prow", "pcol", None),
        P("prow", "pcol", None),
    )
    return jax.shard_map(
        functools.partial(per_device, mesh.shape["prow"], mesh.shape["pcol"]),
        mesh=mesh,
        in_specs=placed,
        out_specs=(
            P("prow", "pcol", None, None, None),
            P("prow", None, None),
            P("pcol", None, None),
            P(),
        ),
        check_vma=False,
    )
```

```python
import functools

import jax
import jax.numpy as jnp
from jax import lax
from jax.experimental import pallas as pl
from jax.experimental.pallas import tpu as pltpu
from jax.sharding import PartitionSpec as P


PASSES = 2
F32, BF = jnp.float32, jnp.bfloat16
VMEM = pl.BlockSpec(memory_space=pltpu.VMEM)
SMEM = pl.BlockSpec(memory_space=pltpu.SMEM)
HBM = pl.BlockSpec(memory_space=pltpu.HBM)


def by(rows, weights):
    return lax.dot_general(rows, weights, (((1,), (0,)), ((), ())), preferred_element_type=F32)


def by_t(rows, weights):
    return lax.dot_general(rows, weights, (((1,), (1,)), ((), ())), preferred_element_type=F32)


def fill_ancestors(parents, ancestors, leaves):
    ancestors[leaves] = 0
    for b in reversed(range(leaves)):
        ancestors[b] = jnp.left_shift(1, parents[b]) | ancestors[parents[b]]


def reach(ancestors, a, b):
    return (jnp.right_shift(ancestors[b], a) & 1).astype(F32)


def mask_of(widths, a, size):
    return (lax.broadcasted_iota(jnp.int32, (1, size), 1) < widths[a]).astype(F32)


def pair(a, b):
    return a * (a - 1) // 2 + b


LINKS = ("band", "strip", "summit")
NAMES = ("inverse", "pair") + LINKS


def forward(w, leaves, source, widths, ancestors, pending, totals, solved):
    size = pending.shape[2]

    def push(a, b, rows):
        term = reach(ancestors, a, b) * by_t(rows, w["pair"][pair(a, b)])
        if b:
            pending[a] += term
        else:
            pending[a] = term

    def links(b):
        for i, name in enumerate(LINKS):
            term = by_t(solved[b], w[name][b])
            if b:
                totals[i] += term
            else:
                totals[i] = term

    for b in range(leaves):
        mask = mask_of(widths, b, size)
        rows = source(b)
        if b:
            rows = rows - pending[b]
        rows = (mask * rows).astype(BF)
        rows = (mask * by_t(rows, w["inverse"][b])).astype(BF)
        solved[b] = rows
        if b:
            for a in range(b + 1, leaves):
                push(a, b - 1, solved[b - 1])
            links(b - 1)
        if b + 1 < leaves:
            push(b + 1, b, rows)
    links(leaves - 1)


def backward(w, leaves, tops, solved, widths, ancestors, pending, answer):
    size = pending.shape[2]

    def outer(a):
        return sum(by(top, w[name][a]) for top, name in zip(tops, LINKS))

    def push(a, b, rows):
        pending[b] += reach(ancestors, a, b) * by(rows, w["pair"][pair(a, b)])

    pending[leaves - 1] = outer(leaves - 1)
    for a in reversed(range(leaves)):
        mask = mask_of(widths, a, size)
        rows = (mask * (solved[a].astype(F32) - pending[a])).astype(BF)
        rows = (mask * by(rows, w["inverse"][a])).astype(BF)
        answer[a] = rows
        if a:
            pending[a - 1] = outer(a - 1) if a == leaves - 1 else pending[a - 1] + outer(a - 1)
            push(a, a - 1, rows)
        for b in range(a - 1):
            term = reach(ancestors, a, b) * by(rows, w["pair"][pair(a, b)])
            if a == leaves - 1:
                pending[b] = term
            else:
                pending[b] += term


def send_pieces(totals, sources, outs):
    peers = len(outs)
    part = totals.shape[1] // peers
    r, c = lax.axis_index("prow"), lax.axis_index("pcol")
    counted = (c == 0, r == 0, (r == 0) & (c == 0))
    for i, (here, source) in enumerate(zip(counted, sources)):

        @pl.when(here)
        def _(i=i, source=source):
            totals[i] -= source

    for m, out in enumerate(outs):
        rows = pl.ds(pl.multiple_of((c ^ m) * part, part), part)
        for i in range(3):
            out[pl.ds(i * part, part)] = totals[i, rows]


def join_pieces(pieces, tops):
    part = tops.shape[1] // len(pieces)
    for m, piece in enumerate(pieces):
        rows = pl.ds(pl.multiple_of((lax.axis_index("pcol") ^ m) * part, part), part)
        for i in range(3):
            tops[i, rows] = piece[pl.ds(i * part, part)]


def first_kernel(n, parents, widths, leaf_source, band_source, strip_source, summit_source, *refs):
    sources, outs, solved, (pending, totals, ancestors) = refs[:5], refs[5 : 5 + n], refs[5 + n], refs[6 + n :]
    w = dict(zip(NAMES, sources))
    leaves = leaf_source.shape[0]
    fill_ancestors(parents, ancestors, leaves)
    forward(w, leaves, lambda b: leaf_source[b].astype(F32).T, widths, ancestors, pending, totals, solved)
    send_pieces(totals, [ref[...].astype(F32).T for ref in (band_source, strip_source, summit_source)], outs)


def middle_kernel(n, last, parents, widths, solved_from, *refs):
    pieces, sources, refs = refs[:n], refs[n : n + 5], refs[n + 5 :]
    if last:
        leaf_answer, *top_answers = refs[:4]
        refs = refs[4:]
    else:
        outs, solved, refs = refs[:n], refs[n], refs[n + 1 :]
    pending, totals, tops, answer, solved_before, ancestors, sem = refs
    w = dict(zip(NAMES, sources))
    leaves = solved_before.shape[0]
    copy = pltpu.make_async_copy(solved_from, solved_before, sem)
    copy.start()
    fill_ancestors(parents, ancestors, leaves)
    join_pieces(pieces, tops)
    rows = [tops[i].astype(BF) for i in range(3)]
    copy.wait()
    backward(w, leaves, rows, solved_before, widths, ancestors, pending, answer)
    if last:
        for a in range(leaves):
            leaf_answer[a] = answer[a].astype(F32).T.astype(BF)
        for i, out in enumerate(top_answers):
            out[...] = tops[i].T.astype(BF)
    else:
        forward(w, leaves, lambda b: answer[b].astype(F32), widths, ancestors, pending, totals, solved)
        send_pieces(totals, [tops[i] for i in range(3)], outs)


def band_kernel(n, inverse, lift, *refs):
    pieces, links, (solved, keep, send), (both,) = refs[:n], refs[n : 2 * n], refs[2 * n : 2 * n + 3], refs[2 * n + 3 :]
    part = solved.shape[0]
    half = keep.shape[0]

    def block(piece, i):
        return piece[pl.ds(i * part, part)]

    partial = sum(block(piece, 0) for piece in pieces)
    rows = by_t((-partial).astype(BF), inverse[...]).astype(BF)
    solved[...] = rows
    for m in range(n):
        both[pl.ds(m * part, part)] = block(pieces[m], 1) + by_t(rows, links[m][...])
    both[pl.ds(n * part, part)] = sum(block(piece, 2) for piece in pieces) + by(rows, lift[...])
    if 2 * half > (n + 1) * part:
        both[pl.ds((n + 1) * part, 2 * half - (n + 1) * part)] = jnp.zeros((2 * half - (n + 1) * part, both.shape[1]), F32)
    core = (lax.axis_index("prow") & 1)
    keep[...] = both[pl.ds(pl.multiple_of(core * half, 8), half)]
    send[...] = both[pl.ds(pl.multiple_of((1 - core) * half, 8), half)]


def top_kernel(n, inverse, lift, summit_inverse, solved, mine, other, *refs):
    links, inverses, lifts = refs[:n], refs[n : 2 * n], refs[2 * n : 3 * n]
    outs, (both,) = refs[3 * n : 4 * n], refs[4 * n :]
    half = mine.shape[0]
    part = solved.shape[0]
    core = (lax.axis_index("prow") & 1)
    both[pl.ds(pl.multiple_of(core * half, 8), half)] = mine[...]
    both[pl.ds(pl.multiple_of((1 - core) * half, 8), half)] = other[...]
    strips = [
        by_t((-both[pl.ds(m * part, part)]).astype(BF), inverses[m][...]).astype(BF) for m in range(n)
    ]
    partial = both[pl.ds(n * part, part)] + sum(by(strips[m], lifts[m][...]) for m in range(n))
    summit = by_t((-partial).astype(BF), summit_inverse[...]).astype(BF)
    summit = by(summit, summit_inverse[...]).astype(BF)
    answers = [
        by((strips[m].astype(F32) - by_t(summit, lifts[m][...])).astype(BF), inverses[m][...]).astype(BF)
        for m in range(n)
    ]
    back = by_t(summit, lift[...]) + sum(by(answers[m], links[m][...]) for m in range(n))
    band = by((solved[...].astype(F32) - back).astype(BF), inverse[...]).astype(BF)
    for m in range(n):
        outs[m][pl.ds(0, part)] = band.astype(F32)
        outs[m][pl.ds(part, part)] = answers[m].astype(F32)
        outs[m][pl.ds(2 * part, part)] = summit.astype(F32)


def place_kernel(core):
    core[...] = jnp.full(core.shape, lax.axis_index("prow") & 1, jnp.int32)


def gather_kernel(n, own, own_inverse, slab, *refs):
    pieces, links, (lift, link, inverse) = refs[: n - 1], refs[n - 1 : 2 * n - 2], refs[2 * n - 2 :]
    link[...] = own[...]
    inverse[...] = own_inverse[...]
    rows = slab.shape[0]
    size = lift.shape[0]
    for m in range(n):
        spot = pl.ds(pl.multiple_of((lax.axis_index("pcol") ^ m) * rows, rows), rows)
        if m:
            links[m - 1][...] = pieces[m - 1][pl.ds(0, size)].astype(BF)
            lift[spot] = pieces[m - 1][pl.ds(size, rows)].astype(BF)
        else:
            lift[spot] = slab[...]


def sort_kernel(n, *refs):
    k = n - 1
    own, refs = refs[:3], refs[3:]
    mine, other, inverses, lifts = refs[:k], refs[k : 2 * k], refs[2 * k : 3 * k], refs[3 * k : 4 * k]
    for out, value in zip(refs[4 * k :], own):
        out[...] = value[...]

    @pl.when((lax.axis_index("prow") & 1) == 0)
    def _():
        for m in range(k):
            inverses[m][...] = mine[m][...].astype(BF)
            lifts[m][...] = other[m][...].astype(BF)

    @pl.when((lax.axis_index("prow") & 1) == 1)
    def _():
        for m in range(k):
            inverses[m][...] = other[m][...].astype(BF)
            lifts[m][...] = mine[m][...].astype(BF)


def cost(flops, moved):
    return pl.CostEstimate(flops=int(flops), bytes_accessed=int(moved), transcendentals=0)


def shape_of(shape, dtype):
    return jax.ShapeDtypeStruct(tuple(shape), dtype)


def swap(array, axis, mask, size):
    return lax.ppermute(array, axis, [(i, i ^ mask) for i in range(size)])


def spread(arrays, size):
    order = sorted(range(1, size), key=lambda m: -bin(m).count("1"))
    got = {m: swap(arrays[m - 1], "pcol", m, size) for m in order}
    return [got[m] for m in range(1, size)]


def inner(
    n_prow,
    n,
    leaf_source,
    band_source,
    strip_source,
    summit_source,
    leaf_inverse,
    band_inverse,
    strip_inverse,
    summit_inverse,
    leaf_blocks,
    band_blocks,
    strip_blocks,
    summit_blocks,
    coupling,
    summit_band,
    summit_strip,
    parents,
    widths,
):
    leaves, size, vectors = leaf_source.shape[2:]
    pairs = leaf_blocks.shape[2]
    part = vectors // n
    half = -(-(n + 1) * part // 16) * 8
    block = (size, size)
    leaf_weights = (leaf_inverse[0, 0], leaf_blocks[0, 0], band_blocks[0, 0], strip_blocks[0, 0], summit_blocks[0, 0])
    small = pltpu.CompilerParams(vmem_limit_bytes=16 * 2**20)
    scratch = [pltpu.VMEM((leaves, vectors, size), F32), pltpu.VMEM((3, vectors, size), F32)]
    ends = [pltpu.SMEM((leaves + 1,), jnp.int32)]
    pieces = [shape_of((3 * part, size), F32)] * n
    solved_shape = shape_of((leaves, vectors, size), BF)
    sweep_flops = 2 * vectors * size * size * (pairs + 4 * leaves)
    weight_bytes = 2 * size * size * (pairs + 4 * leaves)
    lists = (parents[0, 0], widths[0, 0])

    place = pl.pallas_call(
        place_kernel,
        out_shape=shape_of((8, 128), jnp.int32),
        out_specs=VMEM,
        cost_estimate=cost(20 * sweep_flops, weight_bytes),
        compiler_params=small,
        name="place",
    )()
    own_link, own_slab, place = lax.optimization_barrier((coupling[0, 0], summit_band[0], place))
    link_out = jnp.concatenate([own_link, own_slab], 0).astype(F32)
    strip_out = jnp.where(place[0, 0] == 0, strip_inverse[0], summit_strip[0]).astype(F32)
    link_in = spread([link_out] * (n - 1), n)

    *sent, solved = pl.pallas_call(
        functools.partial(first_kernel, n),
        out_shape=pieces + [solved_shape],
        in_specs=[SMEM] * 2 + [VMEM] * 9,
        out_specs=[VMEM] * (n + 1),
        scratch_shapes=scratch + ends,
        cost_estimate=cost(sweep_flops, weight_bytes),
        compiler_params=small,
        name="first_sweep",
    )(*lists, leaf_source[0, 0], band_source[0], strip_source[0], summit_source, *leaf_weights)

    *links, lift, link, band_inverse = pl.pallas_call(
        functools.partial(gather_kernel, n),
        out_shape=[shape_of(block, BF)] * (n + 2),
        in_specs=[VMEM] * (n + 2),
        out_specs=[VMEM] * (n + 2),
        cost_estimate=cost(0, 6 * n * size * size),
        compiler_params=small, name="gather_links",
    )(coupling[0, 0], band_inverse[0], summit_band[0], *link_in)
    links = [link] + links

    for step in range(PASSES):
        last = step == PASSES - 1
        got = list(sent[:1]) + spread(sent[1:], n)
        if step == 0:
            strip_in = spread([strip_out] * (n - 1), n)
            strip_over = [swap(array, "prow", 1, n_prow) for array in strip_in]
            sorted_in = pl.pallas_call(
                functools.partial(sort_kernel, n),
                out_shape=[shape_of(block, BF)] * (2 * n + 1),
                in_specs=[VMEM] * (2 * n + 1),
                out_specs=[VMEM] * (2 * n + 1),
                cost_estimate=cost(0, 12 * n * size * size),
                compiler_params=small, name="sort_strips",
            )(strip_inverse[0], summit_strip[0], summit_inverse, *strip_in, *strip_over)
            inverses = [sorted_in[2 * n - 2]] + list(sorted_in[: n - 1])
            lifts = [sorted_in[2 * n - 1]] + list(sorted_in[n - 1 : 2 * n - 2])
            summit_inverse = sorted_in[2 * n]
        band_solved, keep, send = pl.pallas_call(
            functools.partial(band_kernel, n),
            out_shape=[shape_of((part, size), BF)] + [shape_of((half, size), F32)] * 2,
            in_specs=[VMEM] * (2 * n + 2),
            out_specs=[VMEM] * 3,
            scratch_shapes=[pltpu.VMEM((2 * half, size), F32)],
            cost_estimate=cost(2 * part * size * size * (n + 2), 2 * size * size * (n + 2)),
            compiler_params=small, name="band_solve",
        )(band_inverse, lift, *got, *links)
        mine = keep + swap(send, "prow", 1, n_prow)
        mask = 2
        while mask < n_prow:
            mine = mine + swap(mine, "prow", mask, n_prow)
            mask *= 2
        other = swap(mine, "prow", 1, n_prow)
        back = pl.pallas_call(
            functools.partial(top_kernel, n),
            out_shape=pieces,
            in_specs=[VMEM] * (6 + 3 * n),
            out_specs=[VMEM] * n,
            scratch_shapes=[pltpu.VMEM((2 * half, size), F32)],
            cost_estimate=cost(2 * part * size * size * (5 * n + 4), 2 * size * size * (3 * n + 3)),
            compiler_params=small, name="top_solve",
        )(band_inverse, lift, summit_inverse, band_solved, mine, other, *links, *inverses, *lifts)
        tops = list(back[:1]) + spread(back[1:], n)
        if last:
            shapes = [shape_of((leaves, size, vectors), BF)] + [shape_of((size, vectors), BF)] * 3
        else:
            shapes = pieces + [solved_shape]
        results = pl.pallas_call(
            functools.partial(middle_kernel, n, last),
            out_shape=shapes,
            in_specs=[SMEM] * 2 + [HBM] + [VMEM] * (n + 5),
            out_specs=[VMEM] * len(shapes),
            scratch_shapes=scratch
            + [pltpu.VMEM((3, vectors, size), F32)]
            + [pltpu.VMEM((leaves, vectors, size), BF)] * 2
            + ends
            + [pltpu.SemaphoreType.DMA],
            cost_estimate=cost(sweep_flops * (1 if last else 2), weight_bytes),
            compiler_params=small,
            name="last_sweep" if last else "middle_sweep",
        )(*lists, solved, *tops, *leaf_weights)
        if not last:
            *sent, solved = results
    leaf_answer, band_answer, strip_answer, summit_answer = results
    return leaf_answer[None, None], band_answer[None], strip_answer[None], summit_answer


def solution(mesh):
    placed = (
        P("prow", "pcol", None, None, None),
        P("prow", None, None),
        P("pcol", None, None),
        P(),
        P("prow", "pcol", None, None, None),
        P("prow", None, None),
        P("pcol", None, None),
        P(),
        P("prow", "pcol", None, None, None),
        P("prow", "pcol", None, None, None),
        P("prow", "pcol", None, None, None),
        P("prow", "pcol", None, None, None),
        P("prow", "pcol", None, None),
        P("prow", "pcol", None),
        P("pcol", None, None),
        P("prow", "pcol", None),
        P("prow", "pcol", None),
    )
    return jax.shard_map(
        functools.partial(inner, mesh.shape["prow"], mesh.shape["pcol"]),
        mesh=mesh,
        in_specs=placed,
        out_specs=(
            P("prow", "pcol", None, None, None),
            P("prow", None, None),
            P("pcol", None, None),
            P(),
        ),
        check_vma=False,
    )
```

```python
import functools

import jax
import jax.numpy as jnp
from jax import lax
from jax.experimental import pallas as pl
from jax.experimental.pallas import tpu as pltpu
from jax.sharding import PartitionSpec as P


PASSES = 2
FEW = 4
F32, BF = jnp.float32, jnp.bfloat16
VMEM = pl.BlockSpec(memory_space=pltpu.VMEM)
SMEM = pl.BlockSpec(memory_space=pltpu.SMEM)
HBM = pl.BlockSpec(memory_space=pltpu.HBM)


def by(rows, weights):
    return lax.dot_general(rows, weights, (((1,), (0,)), ((), ())), preferred_element_type=F32)


def by_t(rows, weights):
    return lax.dot_general(rows, weights, (((1,), (1,)), ((), ())), preferred_element_type=F32)


def fill_ancestors(parents, ancestors, leaves):
    ancestors[leaves] = 0
    for b in reversed(range(leaves)):
        ancestors[b] = jnp.left_shift(1, parents[b]) | ancestors[parents[b]]


def reach(ancestors, a, b):
    return (jnp.right_shift(ancestors[b], a) & 1).astype(F32)


def mask_of(widths, a, size):
    return (lax.broadcasted_iota(jnp.int32, (1, size), 1) < widths[a]).astype(F32)


def pair(a, b):
    return a * (a - 1) // 2 + b


LINKS = ("band", "strip", "summit")
NAMES = ("inverse", "pair") + LINKS


def forward(w, leaves, source, widths, ancestors, pending, totals, solved):
    size = pending.shape[2]

    def push(a, b, rows):
        term = reach(ancestors, a, b) * by_t(rows, w["pair"][pair(a, b)])
        if b:
            pending[a] += term
        else:
            pending[a] = term

    def links(b):
        for i, name in enumerate(LINKS):
            term = by_t(solved[b], w[name][b])
            if b:
                totals[i] += term
            else:
                totals[i] = term

    for b in range(leaves):
        mask = mask_of(widths, b, size)
        rows = source(b)
        if b:
            rows = rows - pending[b]
        rows = (mask * rows).astype(BF)
        rows = (mask * by_t(rows, w["inverse"][b])).astype(BF)
        solved[b] = rows
        if b:
            for a in range(b + 1, leaves):
                push(a, b - 1, solved[b - 1])
            links(b - 1)
        if b + 1 < leaves:
            push(b + 1, b, rows)
    links(leaves - 1)


def invert_kernel(first, parents, widths, inverse, pairs, *refs):
    stack, scaled, terms, ancestors = refs[-4:]
    leaves, size = inverse.shape[:2]
    rows_here = scaled.shape[0]
    fill_ancestors(parents, ancestors, leaves)

    def span(first, last):
        return pl.ds(first * size, (last - first) * size)

    for i in range(rows_here):
        a = first + i
        mask = mask_of(widths, a, size)
        rows = (lax.broadcasted_iota(jnp.int32, (size, 1), 0) < widths[a]).astype(F32)
        stack[a, span(a, a + 1)] = (rows * inverse[a].astype(F32) * mask).astype(BF)
        for k in range(a):
            weight = jnp.full((1, size), reach(ancestors, a, k), F32).astype(BF)
            scaled[i, :, span(k, k + 1)] = pairs[pair(a, k)] * weight
    for i in range(rows_here):
        a = first + i
        if not a:
            continue
        for b in reversed(range(a)):
            terms[:, span(b, b + 1)] = by(scaled[i, :, span(b, a)], stack[b, span(b, a)]).astype(BF)
        rows = -by(stack[a, span(a, a + 1)], terms[:, span(0, a)])
        for b in range(a):
            stack[b, span(a, a + 1)] = rows[:, b * size : (b + 1) * size].astype(BF)


def forward_again(stack, links, source, totals, solved):
    leaves, size = stack.shape[0], stack.shape[2]
    for a in range(leaves):
        rows = sum(by_t(source(b), stack[b, pl.ds(a * size, size)]) for b in range(a + 1))
        solved[a] = rows.astype(BF)
    for i, link in enumerate(links):
        totals[i] = sum(by_t(solved[a], link[a]) for a in range(leaves))


def backward(stack, links, tops, solved, residual, put):
    leaves, size = stack.shape[0], stack.shape[2]
    for a in reversed(range(leaves)):
        outer = sum(by(top, link[a]) for top, link in zip(tops, links))
        residual[:, pl.ds(a * size, size)] = (solved[a].astype(F32) - outer).astype(BF)
        rest = pl.ds(a * size, (leaves - a) * size)
        put(a, by(residual[:, rest], stack[a, rest]).astype(BF))


def send_pieces(totals, sources, outs):
    peers = len(outs)
    part = totals.shape[1] // peers
    r, c = lax.axis_index("prow"), lax.axis_index("pcol")
    counted = (c == 0, r == 0, (r == 0) & (c == 0))
    for i, (here, source) in enumerate(zip(counted, sources)):

        @pl.when(here)
        def _(i=i, source=source):
            totals[i] -= source

    for m, out in enumerate(outs):
        rows = pl.ds(pl.multiple_of((c ^ m) * part, part), part)
        for i in range(3):
            out[pl.ds(i * part, part)] = totals[i, rows]


def join_pieces(pieces, tops):
    part = tops.shape[1] // len(pieces)
    for m, piece in enumerate(pieces):
        rows = pl.ds(pl.multiple_of((lax.axis_index("pcol") ^ m) * part, part), part)
        for i in range(3):
            tops[i, rows] = piece[pl.ds(i * part, part)]


def first_kernel(n, parents, widths, leaf_source, band_source, strip_source, summit_source, *refs):
    sources, outs, solved, (pending, totals, ancestors) = refs[:5], refs[5 : 5 + n], refs[5 + n], refs[6 + n :]
    w = dict(zip(NAMES, sources))
    leaves = leaf_source.shape[0]
    fill_ancestors(parents, ancestors, leaves)
    forward(w, leaves, lambda b: leaf_source[b].astype(F32).T, widths, ancestors, pending, totals, solved)
    send_pieces(totals, [ref[...].astype(F32).T for ref in (band_source, strip_source, summit_source)], outs)


def middle_kernel(n, last, solved_before, *refs):
    pieces, stack, links, refs = refs[:n], refs[n], refs[n + 1 : n + 4], refs[n + 4 :]
    if last:
        leaf_answer, *top_answers = refs[:4]
        tops, residual = refs[4:]
    else:
        outs, solved, (tops, residual, answer, totals) = refs[:n], refs[n], refs[n + 1 :]
    join_pieces(pieces, tops)

    def put(a, rows):
        if last:
            leaf_answer[a] = rows.astype(F32).T.astype(BF)
        else:
            answer[a] = rows

    backward(stack, links, [tops[i].astype(BF) for i in range(3)], solved_before, residual, put)
    if last:
        for i, out in enumerate(top_answers):
            out[...] = tops[i].T.astype(BF)
    else:
        forward_again(stack, links, lambda b: answer[b], totals, solved)
        send_pieces(totals, [tops[i] for i in range(3)], outs)


def band_kernel(n, inverse, lift, *refs):
    pieces, links, (solved, keep, send), (both,) = refs[:n], refs[n : 2 * n], refs[2 * n : 2 * n + 3], refs[2 * n + 3 :]
    part = solved.shape[0]
    half = keep.shape[0]

    def block(piece, i):
        return piece[pl.ds(i * part, part)]

    partial = sum(block(piece, 0) for piece in pieces)
    rows = by_t((-partial).astype(BF), inverse[...]).astype(BF)
    solved[...] = rows
    for m in range(n):
        both[pl.ds(m * part, part)] = block(pieces[m], 1) + by_t(rows, links[m][...])
    both[pl.ds(n * part, part)] = sum(block(piece, 2) for piece in pieces) + by(rows, lift[...])
    if 2 * half > (n + 1) * part:
        both[pl.ds((n + 1) * part, 2 * half - (n + 1) * part)] = jnp.zeros((2 * half - (n + 1) * part, both.shape[1]), F32)
    core = (lax.axis_index("prow") & 1)
    keep[...] = both[pl.ds(pl.multiple_of(core * half, 8), half)]
    send[...] = both[pl.ds(pl.multiple_of((1 - core) * half, 8), half)]


def top_kernel(n, inverse, lift, summit_inverse, solved, mine, other, *refs):
    links, inverses, lifts = refs[:n], refs[n : 2 * n], refs[2 * n : 3 * n]
    outs, (both,) = refs[3 * n : 4 * n], refs[4 * n :]
    half = mine.shape[0]
    part = solved.shape[0]
    core = (lax.axis_index("prow") & 1)
    both[pl.ds(pl.multiple_of(core * half, 8), half)] = mine[...]
    both[pl.ds(pl.multiple_of((1 - core) * half, 8), half)] = other[...]
    strips = [
        by_t((-both[pl.ds(m * part, part)]).astype(BF), inverses[m][...]).astype(BF) for m in range(n)
    ]
    partial = both[pl.ds(n * part, part)] + sum(by(strips[m], lifts[m][...]) for m in range(n))
    summit = by_t((-partial).astype(BF), summit_inverse[...]).astype(BF)
    summit = by(summit, summit_inverse[...]).astype(BF)
    answers = [
        by((strips[m].astype(F32) - by_t(summit, lifts[m][...])).astype(BF), inverses[m][...]).astype(BF)
        for m in range(n)
    ]
    back = by_t(summit, lift[...]) + sum(by(answers[m], links[m][...]) for m in range(n))
    band = by((solved[...].astype(F32) - back).astype(BF), inverse[...]).astype(BF)
    for m in range(n):
        outs[m][pl.ds(0, part)] = band.astype(F32)
        outs[m][pl.ds(part, part)] = answers[m].astype(F32)
        outs[m][pl.ds(2 * part, part)] = summit.astype(F32)


def place_kernel(core):
    core[...] = jnp.full(core.shape, lax.axis_index("prow") & 1, jnp.int32)


def gather_kernel(counts, own, own_inverse, slab, *refs):
    n = len(counts) + 1
    pieces, refs = group(refs, counts)
    links, (lift, link, inverse) = refs[: n - 1], refs[n - 1 :]
    link[...] = own[...]
    inverse[...] = own_inverse[...]
    rows = slab.shape[0]
    size = lift.shape[0]
    for m in range(n):
        spot = pl.multiple_of((lax.axis_index("pcol") ^ m) * rows, rows)
        if m:
            put_rows(links[m - 1], 0, pieces[m - 1], 0, size)
            put_rows(lift, spot, pieces[m - 1], size, size + rows)
        else:
            lift[pl.ds(spot, rows)] = slab[...]


def sort_kernel(counts, *refs):
    own, refs = refs[:3], refs[3:]
    k = len(counts)
    mine, refs = group(refs, counts)
    other, refs = group(refs, counts)
    inverses, lifts = refs[:k], refs[k : 2 * k]
    for out, value in zip(refs[2 * k :], own):
        out[...] = value[...]
    for core, (first, second) in enumerate(((mine, other), (other, mine))):

        @pl.when((lax.axis_index("prow") & 1) == core)
        def _(first=first, second=second):
            for m in range(k):
                put_rows(inverses[m], 0, first[m], 0, inverses[m].shape[0])
                put_rows(lifts[m], 0, second[m], 0, lifts[m].shape[0])


def cost(flops, moved):
    return pl.CostEstimate(flops=int(flops), bytes_accessed=int(moved), transcendentals=0)


def shape_of(shape, dtype):
    return jax.ShapeDtypeStruct(tuple(shape), dtype)


def swap(array, axis, mask, size):
    return lax.ppermute(array, axis, [(i, i ^ mask) for i in range(size)])


def spread(arrays, size):
    order = sorted(range(1, size), key=lambda m: -bin(m).count("1"))
    got = {m: swap(arrays[m - 1], "pcol", m, size) for m in order}
    return [got[m] for m in range(1, size)]


def gather(array, size):
    got = {}
    half = array.shape[0] // 2
    for m in sorted(range(1, size), key=lambda m: bin(m).count("1")):
        low, high = m & -m, 1 << (m.bit_length() - 1)
        if low == high:
            got[m] = (swap(array, "pcol", m, size),)
            continue
        near, far = got[m ^ low], got[m ^ high]
        top = near[0][:half] if len(near) == 1 else near[0]
        rest = far[0][half:] if len(far) == 1 else far[1]
        got[m] = (swap(top, "pcol", low, size), swap(rest, "pcol", high, size))
    return [got[m] for m in range(1, size)]


def read_parts(parts):
    def read(first, last):
        out, start = [], 0
        for part in parts:
            end = start + part.shape[0]
            if first < end and last > start:
                out.append((max(first, start) - first, part, max(first, start) - start, min(last, end) - max(first, start)))
            start = end
        return out

    return read


def put_rows(out, base, parts, first, last):
    for offset, part, start, count in read_parts(parts)(first, last):
        out[pl.ds(base + offset, count)] = part[pl.ds(start, count)].astype(BF)


def group(refs, counts):
    out, i = [], 0
    for count in counts:
        out.append(refs[i : i + count])
        i += count
    return out, refs[i:]


def inner(
    n_prow,
    n,
    leaf_source,
    band_source,
    strip_source,
    summit_source,
    leaf_inverse,
    band_inverse,
    strip_inverse,
    summit_inverse,
    leaf_blocks,
    band_blocks,
    strip_blocks,
    summit_blocks,
    coupling,
    summit_band,
    summit_strip,
    parents,
    widths,
):
    leaves, size, vectors = leaf_source.shape[2:]
    pairs = leaf_blocks.shape[2]
    part = vectors // n
    half = -(-(n + 1) * part // 16) * 8
    block = (size, size)
    leaf_weights = (leaf_inverse[0, 0], leaf_blocks[0, 0], band_blocks[0, 0], strip_blocks[0, 0], summit_blocks[0, 0])
    small = pltpu.CompilerParams(vmem_limit_bytes=16 * 2**20)
    scratch = [pltpu.VMEM((leaves, vectors, size), F32), pltpu.VMEM((3, vectors, size), F32)]
    ends = [pltpu.SMEM((leaves + 1,), jnp.int32)]
    pieces = [shape_of((3 * part, size), F32)] * n
    solved_shape = shape_of((leaves, vectors, size), BF)
    sweep_flops = 2 * vectors * size * size * (pairs + 4 * leaves)
    weight_bytes = 2 * size * size * (pairs + 4 * leaves)
    lists = (parents[0, 0], widths[0, 0])

    place = pl.pallas_call(
        place_kernel,
        out_shape=shape_of((8, 128), jnp.int32),
        out_specs=VMEM,
        cost_estimate=cost(20 * sweep_flops, weight_bytes),
        compiler_params=small,
        name="place",
    )()
    own_link, own_slab, place = lax.optimization_barrier((coupling[0, 0], summit_band[0], place))
    link_out = jnp.concatenate([own_link, own_slab], 0).astype(F32)
    strip_out = jnp.where(place[0, 0] == 0, strip_inverse[0], summit_strip[0]).astype(F32)
    link_in = gather(link_out, n)
    counts = [len(parts) for parts in link_in]

    *sent, solved = pl.pallas_call(
        functools.partial(first_kernel, n),
        out_shape=pieces + [solved_shape],
        in_specs=[SMEM] * 2 + [VMEM] * 9,
        out_specs=[VMEM] * (n + 1),
        scratch_shapes=scratch + ends,
        cost_estimate=cost(sweep_flops, weight_bytes),
        compiler_params=small,
        name="first_sweep",
    )(*lists, leaf_source[0, 0], band_source[0], strip_source[0], summit_source, *leaf_weights)

    cut = leaves - leaves // 4

    def invert(first, last, *stack):
        return pl.pallas_call(
            functools.partial(invert_kernel, first),
            out_shape=[shape_of((leaves, leaves * size, size), BF)],
            in_specs=[SMEM] * 2 + [VMEM] * (2 + len(stack)),
            out_specs=[VMEM],
            scratch_shapes=[
                pltpu.VMEM((last - first, size, leaves * size), BF),
                pltpu.VMEM((size, leaves * size), BF),
                pltpu.SMEM((leaves + 1,), jnp.int32),
            ],
            input_output_aliases={4: 0} if stack else {},
            cost_estimate=cost(5 * size**3 * pairs, weight_bytes),
            compiler_params=small,
        )(*lists, *leaf_weights[:2], *stack)[0]

    stack = invert(0, cut)

    *links, lift, link, band_inverse = pl.pallas_call(
        functools.partial(gather_kernel, counts),
        out_shape=[shape_of(block, BF)] * (n + 2),
        in_specs=[VMEM] * (3 + sum(counts)),
        out_specs=[VMEM] * (n + 2),
        cost_estimate=cost(0, 6 * n * size * size),
        compiler_params=small, name="gather_links",
    )(coupling[0, 0], band_inverse[0], summit_band[0], *sum(link_in, ()))
    links = [link] + links

    for step in range(PASSES):
        last = step == PASSES - 1
        got = list(sent[:1]) + spread(sent[1:], n)
        if step == 0:
            strip_in = sum(gather(strip_out, n), ())
            strip_over = [swap(array, "prow", 1, n_prow) for array in strip_in]
            sorted_in = pl.pallas_call(
                functools.partial(sort_kernel, counts),
                out_shape=[shape_of(block, BF)] * (2 * n + 1),
                in_specs=[VMEM] * (3 + 2 * sum(counts)),
                out_specs=[VMEM] * (2 * n + 1),
                cost_estimate=cost(0, 12 * n * size * size),
                compiler_params=small, name="sort_strips",
            )(strip_inverse[0], summit_strip[0], summit_inverse, *strip_in, *strip_over)
            inverses = [sorted_in[2 * n - 2]] + list(sorted_in[: n - 1])
            lifts = [sorted_in[2 * n - 1]] + list(sorted_in[n - 1 : 2 * n - 2])
            summit_inverse = sorted_in[2 * n]
        band_solved, keep, send = pl.pallas_call(
            functools.partial(band_kernel, n),
            out_shape=[shape_of((part, size), BF)] + [shape_of((half, size), F32)] * 2,
            in_specs=[VMEM] * (2 * n + 2),
            out_specs=[VMEM] * 3,
            scratch_shapes=[pltpu.VMEM((2 * half, size), F32)],
            cost_estimate=cost(2 * part * size * size * (n + 2), 2 * size * size * (n + 2)),
            compiler_params=small, name="band_solve",
        )(band_inverse, lift, *got, *links)
        mine = keep + swap(send, "prow", 1, n_prow)
        if step and n_prow // 2 <= FEW:
            terms = [mine] + [swap(mine, "prow", mask, n_prow) for mask in range(2, n_prow, 2)]
            while len(terms) > 1:
                terms = [one + two for one, two in zip(terms[::2], terms[1::2])]
            mine = terms[0]
        else:
            mask = 2
            while mask < n_prow:
                mine = mine + swap(mine, "prow", mask, n_prow)
                mask *= 2
        other = swap(mine, "prow", 1, n_prow)
        back = pl.pallas_call(
            functools.partial(top_kernel, n),
            out_shape=pieces,
            in_specs=[VMEM] * (6 + 3 * n),
            out_specs=[VMEM] * n,
            scratch_shapes=[pltpu.VMEM((2 * half, size), F32)],
            cost_estimate=cost(2 * part * size * size * (5 * n + 4), 2 * size * size * (3 * n + 3)),
            compiler_params=small, name="top_solve",
        )(band_inverse, lift, summit_inverse, band_solved, mine, other, *links, *inverses, *lifts)
        tops = list(back[:1]) + spread(back[1:], n)
        if not last:
            stack = invert(cut, leaves, stack)
        if last:
            shapes = [shape_of((leaves, size, vectors), BF)] + [shape_of((size, vectors), BF)] * 3
        else:
            shapes = pieces + [solved_shape]
        results = pl.pallas_call(
            functools.partial(middle_kernel, n, last),
            out_shape=shapes,
            in_specs=[VMEM] * (n + 5),
            out_specs=[VMEM] * len(shapes),
            scratch_shapes=[pltpu.VMEM((3, vectors, size), F32), pltpu.VMEM((vectors, leaves * size), BF)]
            + ([] if last else [pltpu.VMEM((leaves, vectors, size), BF), pltpu.VMEM((3, vectors, size), F32)]),
            cost_estimate=cost(sweep_flops * (1 if last else 2), weight_bytes),
            compiler_params=small,
            name="last_sweep" if last else "middle_sweep",
        )(solved, *tops, stack, *leaf_weights[2:])
        if not last:
            *sent, solved = results
    leaf_answer, band_answer, strip_answer, summit_answer = results
    return leaf_answer[None, None], band_answer[None], strip_answer[None], summit_answer


def solution(mesh):
    placed = (
        P("prow", "pcol", None, None, None),
        P("prow", None, None),
        P("pcol", None, None),
        P(),
        P("prow", "pcol", None, None, None),
        P("prow", None, None),
        P("pcol", None, None),
        P(),
        P("prow", "pcol", None, None, None),
        P("prow", "pcol", None, None, None),
        P("prow", "pcol", None, None, None),
        P("prow", "pcol", None, None, None),
        P("prow", "pcol", None, None),
        P("prow", "pcol", None),
        P("pcol", None, None),
        P("prow", "pcol", None),
        P("prow", "pcol", None),
    )
    return jax.shard_map(
        functools.partial(inner, mesh.shape["prow"], mesh.shape["pcol"]),
        mesh=mesh,
        in_specs=placed,
        out_specs=(
            P("prow", "pcol", None, None, None),
            P("prow", None, None),
            P("pcol", None, None),
            P(),
        ),
        check_vma=False,
    )
```
